32 devices in a mesh: col: 4 (over z), row: 8 (over y, x, core).
Axes of the slice: x: 2, y: 2, z: 4, core: 2. Of those that a mesh axis runs over, the one named last changes fastest.
Arguments:
- affinity: bfloat16 [3840, 128, 128], P(('col', 'row')), may hold values from 0 to 0.015625
- tile_rows: int32 [3840], P(('col', 'row')), may hold values from 0 to 19
- tile_cols: int32 [3840], P(('col', 'row')), may hold values from 0 to 39
- live_tiles: int32 [32], P(('col', 'row')), may hold values from 1 to 120, as said below
- start: float32 [20480, 256], P(('col', 'row')), may hold values from -1500 to 1500
Outputs:
- vectors: float32 [20480, 256], P(('col', 'row'))
- first_passes: float32 [2, 20480, 256], P(None, ('col', 'row'))
The draws below stay inside these ranges and needn't reach their ends.
Inputs may be any that keep to these rules, and one draw needn't show every extreme that they name: A device's tiles are its slots 0 to live_tiles - 1; later slots are ignored. Some device holds exactly 120 tiles.
All inputs are finite; a program needn't handle non-finite values.
Results may differ from the reference program's by a relative error of at most 0.0003.
Values sent between devices are 32-bit elements; how exact they have to be, the bound alone decides.
No kernel may reach another device: no remote copies, remote signals or barrier semaphores. Data moves between devices by JAX's collectives and lax.ppermute only.
A program may use at most 128 MiB of HBM per device.

```python
import math
import jax
import jax.numpy as jnp
from jax import lax

TILE = 128
VECS = 256
ITERS = 2
TROWS_DEV = 5
NIMG = 20480
SLOTS = 120
ROWSET_T = 20
COLBLK_T = 40
N_ROW = 8
DEVICES = 32


def draw_live_tiles(key, part):
    first_key, second_key, third_key = jax.random.split(key, 3)
    draws_one = jax.random.randint(first_key, (DEVICES,), 1, SLOTS + 1)
    draws_two = jax.random.randint(second_key, (DEVICES,), 1, SLOTS + 1)
    counts = jnp.minimum(draws_one, draws_two)
    busiest = jax.random.randint(third_key, (), 0, DEVICES)
    counts = jnp.where(jnp.arange(DEVICES) == busiest, SLOTS, counts)
    return counts.astype(jnp.int32)


def draw_start(key, part):
    base_key, rows_key, cols_key = jax.random.split(jax.random.fold_in(key, 7), 3)
    base = jnp.clip(jax.random.normal(base_key, (NIMG, VECS), jnp.float32), -5.0, 5.0)
    row_scale = jnp.exp(jax.random.uniform(rows_key, (NIMG, 1), jnp.float32, 0.0, math.log(10.0)))
    rising = jnp.exp(math.log(3.0) * jnp.arange(NIMG, dtype=jnp.float32) / NIMG)[:, None]
    col_scale = jnp.exp(jax.random.uniform(cols_key, (1, VECS), jnp.float32, 0.0, math.log(10.0)))
    return (base * row_scale * rising * col_scale).astype(jnp.float32)


def plant(drawn, own_key, smallest, largest):
    extent = drawn.shape
    index_at = [jax.random.randint(jax.random.fold_in(own_key, axis), (), 0, extent[axis]) for axis in range(len(extent))]
    drawn = drawn.at[tuple(index_at)].set(smallest)
    longest = extent.index(max(extent))
    index_at[longest] = (index_at[longest] + 1) % extent[longest]
    return drawn.at[tuple(index_at)].set(largest)


def levels(stream_key, extent, pieces, low, top_value):
    level, own = 1.0, jax.random.fold_in(stream_key, 6)
    for dim, parts in pieces:
        draws = jnp.exp(jax.random.uniform(jax.random.fold_in(own, dim), (parts,), jnp.float32, low / len(pieces), top_value / len(pieces)))
        level = level * jnp.repeat(draws, extent[dim] // parts).reshape([-1 if axis == dim else 1 for axis in range(len(extent))])
    return level


def setup_inputs(seed: int = 0) -> dict:
    key_list = jax.random.split(jax.random.key(seed), 6)
    affinity = jnp.clip(0.015625 * jax.random.uniform(key_list[0], (DEVICES * SLOTS, TILE, TILE), jnp.float32) ** levels(key_list[0], (DEVICES * SLOTS, TILE, TILE), ((0, 32),), -0.2, 0.2), 0.0, 0.015625).astype(jnp.bfloat16)
    tile_rows = plant(jax.random.randint(key_list[1], (DEVICES * SLOTS,), 0, ROWSET_T), jax.random.fold_in(key_list[1], 1), 0, ROWSET_T - 1).astype(jnp.int32)
    tile_cols = plant(jax.random.randint(key_list[2], (DEVICES * SLOTS,), 0, COLBLK_T), jax.random.fold_in(key_list[2], 1), 0, COLBLK_T - 1).astype(jnp.int32)
    live_tiles = draw_live_tiles(jax.random.fold_in(key_list[5], 71), 0)
    start = draw_start(jax.random.fold_in(key_list[5], 71), 0)
    return dict(affinity=affinity, tile_rows=tile_rows, tile_cols=tile_cols, live_tiles=live_tiles, start=start)


highest = lax.Precision.HIGHEST

def inverse_factor(matrix):
    gram = jnp.dot(matrix.T.astype(jnp.float32), matrix.astype(jnp.float32), precision=highest, preferred_element_type=jnp.float32)
    lower = jnp.linalg.cholesky(gram)
    return jax.scipy.linalg.solve_triangular(lower, jnp.eye(VECS, dtype=jnp.float32), lower=True)

def normalize(matrix):
    return jnp.dot(matrix.astype(jnp.float32), inverse_factor(matrix).T.astype(jnp.float32), precision=highest, preferred_element_type=jnp.float32)

def accumulate(affinity, tile_rows, tile_cols, live_tiles, initial, contribution):

    def device_step(device, totals):
        dev_col = device // N_ROW
        dev_row = device % N_ROW

        def slot_step(slot_number, partial_acc):
            flat_index = device * SLOTS + slot_number
            tile_row = tile_rows[flat_index]
            target = (tile_row // TROWS_DEV * N_ROW + dev_row) * TROWS_DEV + tile_row % TROWS_DEV
            source = dev_col * N_ROW * TROWS_DEV + tile_cols[flat_index]
            square = lax.dynamic_index_in_dim(affinity, flat_index, 0, keepdims=False).astype(jnp.float32)
            current = lax.dynamic_index_in_dim(partial_acc, target, 0, keepdims=False)
            return lax.dynamic_update_index_in_dim(partial_acc, current + contribution(square, source), target, 0)
        return lax.fori_loop(jnp.int32(0), live_tiles[device], slot_step, totals)
    return lax.fori_loop(jnp.int32(0), jnp.int32(DEVICES), device_step, initial)

def row_total(square, source):
    return lax.optimization_barrier(jnp.sum(square, axis=1))

def reference(affinity, tile_rows, tile_cols, live_tiles, start):
    totals = accumulate(affinity, tile_rows, tile_cols, live_tiles, jnp.zeros((NIMG // TILE, TILE), jnp.float32), row_total)
    degree = 1.0 + totals.reshape(NIMG)
    scaling = (1.0 / jnp.sqrt(degree))[:, None]
    basis = start
    firsts = []
    for step_number in range(ITERS):
        scaled = scaling * basis
        tiled_panels = scaled.reshape(NIMG // TILE, TILE, VECS)

        def product(square, source):
            panel_rows = lax.dynamic_index_in_dim(tiled_panels, source, 0, keepdims=False)
            return jnp.dot(square.astype(jnp.float32), panel_rows.astype(jnp.float32), precision=highest, preferred_element_type=jnp.float32)
        image = accumulate(affinity, tile_rows, tile_cols, live_tiles, jnp.zeros((NIMG // TILE, TILE, VECS), jnp.float32), product)
        image_block = scaling * (scaled + image.reshape(NIMG, VECS))
        first = normalize(image_block)
        firsts.append(first)
        basis = normalize(first)
    root = jnp.sqrt(jnp.float32(NIMG))
    return (root * basis, root * jnp.stack(firsts, axis=0))
```

```python
import jax
import jax.numpy as jnp
from jax import lax
from jax.experimental import pallas as pl
from jax.experimental.pallas import tpu as pltpu
from jax.sharding import PartitionSpec as P

ITERS = 2
PANEL = 8
CHUNKS = 2


highest = lax.Precision.HIGHEST


def dot(a, b, dims=((1,), (0,))):
    return lax.dot_general(
        a, b, (dims, ((), ())), precision=highest, preferred_element_type=jnp.float32
    )


def swap(x, axis, d):
    n = lax.axis_size(axis)
    return lax.ppermute(x, axis, [(i, i ^ d) for i in range(n)])


def tree_sum(parts):
    while len(parts) > 1:
        parts = [parts[i] + parts[i + 1] for i in range(0, len(parts), 2)]
    return parts[0]


def gather_row(x):
    n = lax.axis_size("row")
    even = [x] + [swap(x, "row", d) for d in range(2, n, 2)]
    pieces = []
    for p in even:
        pieces += [p, swap(p, "row", 1)]
    return pieces


def product_kernel(n_row, n_col, own, scaled_here):
    def kernel(meta, rows, cols, aff, *refs):
        pieces, refs = refs[:n_row], refs[n_row:]
        if scaled_here:
            factors, refs = refs[0], refs[1:]
        outs, (split, total) = refs[:-2], refs[-2:]
        size, vecs = aff.shape[1], pieces[0].shape[1]
        live, r, c = meta[0], meta[1], meta[2]
        total[...] = jnp.zeros(total.shape, jnp.float32)
        for d in range(n_row):
            first = (r ^ d) * own
            for t in range(own):
                x = pieces[d][t * size : (t + 1) * size, :]
                if scaled_here:
                    x = x * factors[:, d * own + t : d * own + t + 1]
                high = x.astype(jnp.bfloat16)
                low = (x - high.astype(jnp.float32)).astype(jnp.bfloat16)
                split[first + t, :, :vecs] = high
                split[first + t, :, vecs:] = low

        def one(s):
            t = rows[s]
            q = ((t // own) ^ c) * own + t % own
            y = jnp.dot(aff[s], split[cols[s]], preferred_element_type=jnp.float32)
            total[q] = total[q] + (y[:, :vecs] + y[:, vecs:])

        def four(i, carry):
            for j in range(4):
                one(i * 4 + j)
            return carry

        def rest(s, carry):
            one(s)
            return carry

        whole = live // 4
        lax.fori_loop(0, whole, four, 0)
        lax.fori_loop(whole * 4, live, rest, 0)
        for o, qs in zip(outs, out_blocks(n_col)):
            for i, q in enumerate(qs):
                for t in range(own):
                    o[(i * own + t) * size : (i * own + t + 1) * size, :] = total[q * own + t]

    return kernel


def out_blocks(n_col):
    groups = [[0]]
    bit = n_col // 2
    while bit:
        groups.append([q for q in range(bit, n_col, 2 * bit)])
        bit //= 2
    return groups


def tile_products(meta, rows, cols, affinity, pieces, factors, n_col):
    n_row = len(pieces)
    size = affinity.shape[1]
    local, vecs = pieces[0].shape
    own = local // size
    vmem = pl.BlockSpec(memory_space=pltpu.VMEM)
    smem = pl.BlockSpec(memory_space=pltpu.SMEM)
    extra = [] if factors is None else [factors]
    return pl.pallas_call(
        product_kernel(n_row, n_col, own, factors is not None),
        in_specs=[smem] * 3 + [vmem] * (1 + n_row + len(extra)),
        out_specs=[vmem] * len(out_blocks(n_col)),
        out_shape=[
            jax.ShapeDtypeStruct((len(g) * local, vecs), jnp.float32) for g in out_blocks(n_col)
        ],
        scratch_shapes=[
            pltpu.VMEM((n_row * own, size, 2 * vecs), jnp.bfloat16),
            pltpu.VMEM((n_col * own, size, vecs), jnp.float32),
        ],
    )(meta, rows, cols, affinity, *pieces, *extra)


def scatter_col(parts):
    parts = list(parts)
    local = parts[0].shape[0]
    n = len(parts)
    for step in range(n - 1):
        got = swap(parts[-1], "col", 1 << step)
        parts = parts[:-1]
        count = got.shape[0] // local
        place = {i * 2: got[i * local : (i + 1) * local] for i in range(count)}
        groups = out_blocks(count * 2)[: len(parts)] if count > 1 else [[0]]
        new = []
        for p, g in zip(parts, groups):
            new.append(p + jnp.concatenate([place[q] for q in g]) if len(g) > 1 else p + place[g[0]])
        parts = new
    return parts[0]


def base_inverse(a):
    n = a.shape[0]
    groups = n // PANEL
    sub = lax.broadcasted_iota(jnp.int32, (PANEL, n), 0)
    lane = lax.broadcasted_iota(jnp.int32, (PANEL, n), 1)

    def row(x, k):
        return jnp.broadcast_to(x[k : k + 1, :], x.shape)

    def col(x, k):
        return jnp.broadcast_to(x[:, k : k + 1], x.shape)

    left = [a[g * PANEL : (g + 1) * PANEL, :] for g in range(groups)]
    right = [(lane == sub + g * PANEL).astype(jnp.float32) for g in range(groups)]
    for p in range(groups):
        u, v = left[p], right[p]
        c = [col(u, p * PANEL + j) for j in range(PANEL)]
        more = p + 1 < groups
        if more:
            un, vn = left[p + 1], right[p + 1]
            cn = [col(un, p * PANEL + j) for j in range(PANEL)]
        pivots = jnp.ones((PANEL, n), jnp.float32)
        for k in range(PANEL):
            pivot = row(c[k], k)
            inv = 1.0 / pivot
            pivots = jnp.where(sub == k, pivot, pivots)
            uk, vk = row(u, k), row(v, k)
            ck = {j: row(c[j], k) for j in range(k + 1, PANEL)}
            if more:
                m = cn[k] * inv
                un = un - m * uk
                vn = vn - m * vk
                for j in ck:
                    cn[j] = cn[j] - m * ck[j]
            if k + 1 < PANEL:
                m = jnp.where(sub > k, c[k] * inv, 0.0)
                for j in ck:
                    c[j] = c[j] - m * ck[j]
                u = u - m * uk
                v = v - m * vk
        s = lax.rsqrt(pivots)
        s = s * (1.5 - 0.5 * pivots * s * s)
        u, v = u * s, v * s
        right[p] = v
        if p + 2 < groups:
            w = dot(u, jnp.concatenate([u, v], axis=1), ((0,), (0,)))
            for g in range(p + 2, groups):
                part = w[g * PANEL : (g + 1) * PANEL, :]
                left[g] = left[g] - part[:, :n]
                right[g] = right[g] - part[:, n:]
        if more:
            left[p + 1], right[p + 1] = un, vn
    return jnp.concatenate(right, axis=0)


def inverse_kernel(meta, mine, theirs, out, gram):
    r, n_row = meta[1], meta[3]
    j, c = r // 2, r % 2
    n = gram.shape[0]
    half = n // 2
    pieces = mine.shape[0]
    height = mine.shape[1]
    for d in range(pieces):
        at = (j ^ d) * height
        gram[pl.ds(pl.multiple_of(c * half + at, 8), height), :] = mine[d]
        gram[pl.ds(pl.multiple_of((1 - c) * half + at, 8), height), :] = theirs[d]
    first = base_inverse(gram[:half, :half])
    out[:half, :half] = first
    out[:half, half:] = jnp.zeros((half, half), jnp.float32)
    below = dot(gram[half:, :half], first, ((1,), (1,)))
    second = base_inverse(gram[half:, half:] - dot(below, below, ((1,), (1,))))
    out[half:, half:] = second
    out[half:, :half] = -dot(second, dot(below, first))


def inverse_lower(meta, mine, theirs):
    n = mine.shape[2]
    vmem = pl.BlockSpec(memory_space=pltpu.VMEM)
    return pl.pallas_call(
        inverse_kernel,
        in_specs=[pl.BlockSpec(memory_space=pltpu.SMEM), vmem, vmem],
        out_specs=vmem,
        out_shape=jax.ShapeDtypeStruct((n, n), jnp.float32),
        scratch_shapes=[pltpu.VMEM((n, n), jnp.float32)],
    )(meta, mine, theirs)


def summed_inverse(meta, matrix):
    gram = dot(matrix, matrix, ((0,), (0,)))
    n_row, n_col = lax.axis_size("row"), lax.axis_size("col")
    n = gram.shape[0]
    r = lax.axis_index("row")
    j, c = r // 2, r % 2
    height = n // n_row
    pairs = n_row // 2
    gram = gram + swap(gram, "row", 1)
    parts = []
    for d in range(pairs):
        piece = lax.dynamic_slice_in_dim(gram, (c * pairs + (j ^ d)) * height, height, 0)
        parts.append(swap(piece, "row", 2 * d) if d else piece)
    piece = tree_sum(parts)
    piece = tree_sum([piece] + [swap(piece, "col", d) for d in range(1, n_col)])
    mine = jnp.stack([piece] + [swap(piece, "row", 2 * d) for d in range(1, pairs)])
    return inverse_lower(meta, mine, swap(mine, "row", 1))


def apply_factor(matrix, inverse):
    return dot(matrix, inverse, ((1,), (1,)))


def body(affinity, tile_rows, tile_cols, live_tiles, start):
    n_row = lax.axis_size("row")
    n_col = lax.axis_size("col")
    r = lax.axis_index("row")
    c = lax.axis_index("col")
    slot_count, tile_size = affinity.shape[0], affinity.shape[1]
    rows_local, vec_count = start.shape
    own_tiles = rows_local // tile_size
    width = vec_count // CHUNKS
    meta = jnp.stack([live_tiles[0], r, c, jnp.int32(n_row)]).astype(jnp.int32)

    def chunk(x, i):
        return x[:, i * width : (i + 1) * width]

    gathered = [gather_row(chunk(start, i)) for i in range(CHUNKS)]

    live = (jnp.arange(slot_count) < live_tiles[0]).astype(jnp.float32)
    row_onehot = (jnp.arange(own_tiles * n_col)[:, None] == tile_rows[None, :]).astype(
        jnp.float32
    ) * live[None, :]
    row_sums = jnp.sum(affinity, axis=2, dtype=jnp.float32)
    degree_terms = dot(row_onehot, row_sums).reshape(n_col, own_tiles, tile_size)
    mine = []
    for d in range(n_col):
        block = lax.dynamic_index_in_dim(degree_terms, c ^ d, 0, keepdims=False)
        mine.append(swap(block, "col", d) if d else block)
    scaling_tiles = 1.0 / jnp.sqrt(1.0 + tree_sum(mine))
    factors = jnp.concatenate(
        [scaling_tiles] + [swap(scaling_tiles, "row", d) for d in range(1, n_row)]
    ).T
    scaling = scaling_tiles.reshape(rows_local)[:, None]

    def image_chunk(pieces, scaled, factors):
        parts = tile_products(meta, tile_rows, tile_cols, affinity, pieces, factors, n_col)
        return scaling * (scaled + scatter_col(parts))

    images = []
    for i in range(CHUNKS):
        images.append(image_chunk(gathered[i], scaling * chunk(start, i), factors))
    image = jnp.concatenate(images, axis=1)
    firsts = []
    for step_number in range(1, ITERS):
        nexts = []
        for i in range(CHUNKS):
            scaled = scaling * images[i]
            nexts.append(image_chunk(gather_row(scaled), scaled, None))
        inner = summed_inverse(meta, image)
        first = apply_factor(image, inner)
        firsts.append(first)
        factor = dot(summed_inverse(meta, first), inner)
        image = apply_factor(jnp.concatenate(nexts, axis=1), factor)
        images = [chunk(image, i) for i in range(CHUNKS)]
    pending = apply_factor(image, summed_inverse(meta, image))
    firsts.append(pending)
    basis = apply_factor(pending, summed_inverse(meta, pending))
    total_images = rows_local * n_row * n_col
    root = jnp.sqrt(jnp.float32(total_images))
    return (root * basis, root * jnp.stack(firsts, axis=0))


def solution(mesh):
    placed = (
        P(("col", "row"), None, None),
        P(("col", "row")),
        P(("col", "row")),
        P(("col", "row")),
        P(("col", "row"), None),
    )
    return jax.shard_map(
        body,
        mesh=mesh,
        in_specs=placed,
        out_specs=(P(("col", "row"), None), P(None, ("col", "row"), None)),
        check_vma=False,
    )
```

```python
import jax
import jax.numpy as jnp
from jax import lax
from jax.experimental import pallas as pl
from jax.experimental.pallas import tpu as pltpu
from jax.sharding import PartitionSpec as P

ITERS = 2
PANEL = 8
CHUNKS = 2


highest = lax.Precision.HIGHEST


def dot(a, b, dims=((1,), (0,))):
    return lax.dot_general(
        a, b, (dims, ((), ())), precision=highest, preferred_element_type=jnp.float32
    )


def swap(x, axis, d):
    n = lax.axis_size(axis)
    return lax.ppermute(x, axis, [(i, i ^ d) for i in range(n)])


def tree_sum(parts):
    while len(parts) > 1:
        parts = [parts[i] + parts[i + 1] for i in range(0, len(parts), 2)]
    return parts[0]


def gather_row(x):
    n = lax.axis_size("row")
    return [x] + [swap(x, "row", d) for d in range(2, n, 2)]


def forward(pieces):
    stacked = jnp.stack(pieces)
    return swap(stacked, "row", 1)


def product_kernel(n_row, n_col, own, scaled_here):
    def kernel(meta, rows, cols, aff, *refs):
        mine, theirs, refs = refs[: n_row // 2], refs[n_row // 2], refs[n_row // 2 + 1 :]
        if scaled_here:
            factors, refs = refs[0], refs[1:]
        outs, (split, total) = refs[:-2], refs[-2:]
        size, vecs = aff.shape[1], mine[0].shape[1]
        live, r, c = meta[0], meta[1], meta[2]
        total[...] = jnp.zeros(total.shape, jnp.float32)
        for d in range(n_row):
            first = (r ^ d) * own
            for t in range(own):
                at = slice(t * size, (t + 1) * size)
                x = theirs[d // 2, at, :] if d % 2 else mine[d // 2][at, :]
                if scaled_here:
                    x = x * factors[:, d * own + t : d * own + t + 1]
                high = x.astype(jnp.bfloat16)
                low = (x - high.astype(jnp.float32)).astype(jnp.bfloat16)
                split[first + t, :, :vecs] = high
                split[first + t, :, vecs:] = low

        def one(s):
            t = rows[s]
            q = ((t // own) ^ c) * own + t % own
            y = jnp.dot(aff[s], split[cols[s]], preferred_element_type=jnp.float32)
            total[q] = total[q] + (y[:, :vecs] + y[:, vecs:])

        def four(i, carry):
            for j in range(4):
                one(i * 4 + j)
            return carry

        def rest(s, carry):
            one(s)
            return carry

        whole = live // 4
        lax.fori_loop(0, whole, four, 0)
        lax.fori_loop(whole * 4, live, rest, 0)
        for o, qs in zip(outs, out_blocks(n_col)):
            for i, q in enumerate(qs):
                for t in range(own):
                    o[(i * own + t) * size : (i * own + t + 1) * size, :] = total[q * own + t]

    return kernel


def out_blocks(n_col):
    groups = [[0]]
    bit = n_col // 2
    while bit:
        groups.append([q for q in range(bit, n_col, 2 * bit)])
        bit //= 2
    return groups


def tile_products(meta, rows, cols, affinity, pieces, theirs, factors, n_col):
    n_row = 2 * len(pieces)
    size = affinity.shape[1]
    local, vecs = pieces[0].shape
    own = local // size
    vmem = pl.BlockSpec(memory_space=pltpu.VMEM)
    smem = pl.BlockSpec(memory_space=pltpu.SMEM)
    extra = [] if factors is None else [factors]
    return pl.pallas_call(
        product_kernel(n_row, n_col, own, factors is not None),
        in_specs=[smem] * 3 + [vmem] * (2 + len(pieces) + len(extra)),
        out_specs=[vmem] * len(out_blocks(n_col)),
        out_shape=[
            jax.ShapeDtypeStruct((len(g) * local, vecs), jnp.float32) for g in out_blocks(n_col)
        ],
        scratch_shapes=[
            pltpu.VMEM((n_row * own, size, 2 * vecs), jnp.bfloat16),
            pltpu.VMEM((n_col * own, size, vecs), jnp.float32),
        ],
    )(meta, rows, cols, affinity, *pieces, theirs, *extra)


def scatter_col(parts):
    parts = list(parts)
    local = parts[0].shape[0]
    n = len(parts)
    for step in range(n - 1):
        got = swap(parts[-1], "col", 1 << step)
        parts = parts[:-1]
        if len(parts) == 1:
            return parts[0], got
        count = got.shape[0] // local
        place = {i * 2: got[i * local : (i + 1) * local] for i in range(count)}
        groups = out_blocks(count * 2)[: len(parts)] if count > 1 else [[0]]
        new = []
        for p, g in zip(parts, groups):
            new.append(p + jnp.concatenate([place[q] for q in g]) if len(g) > 1 else p + place[g[0]])
        parts = new


def finish_kernel(scaling, basis, total, more, image, following):
    factor = jnp.broadcast_to(scaling[...], total.shape)
    value = factor * (factor * basis[...] + (total[...] + more[...]))
    image[...] = value
    following[...] = factor * value


def finish(scaling, basis, total, more):
    vmem = pl.BlockSpec(memory_space=pltpu.VMEM)
    shape = jax.ShapeDtypeStruct(total.shape, jnp.float32)
    return pl.pallas_call(
        finish_kernel, in_specs=[vmem] * 4, out_specs=[vmem] * 2, out_shape=[shape] * 2
    )(scaling, basis, total, more)


def base_inverse(a):
    n = a.shape[0]
    groups = n // PANEL
    sub = lax.broadcasted_iota(jnp.int32, (PANEL, n), 0)
    lane = lax.broadcasted_iota(jnp.int32, (PANEL, n), 1)

    def row(x, k):
        return jnp.broadcast_to(x[k : k + 1, :], x.shape)

    def col(x, k):
        return jnp.broadcast_to(x[:, k : k + 1], x.shape)

    left = [a[g * PANEL : (g + 1) * PANEL, :] for g in range(groups)]
    right = [(lane == sub + g * PANEL).astype(jnp.float32) for g in range(groups)]
    for p in range(groups):
        u, v = left[p], right[p]
        c = [col(u, p * PANEL + j) for j in range(PANEL)]
        more = p + 1 < groups
        if more:
            un, vn = left[p + 1], right[p + 1]
            cn = [col(un, p * PANEL + j) for j in range(PANEL)]
        pivots = jnp.ones((PANEL, n), jnp.float32)
        for k in range(PANEL):
            pivot = row(c[k], k)
            inv = 1.0 / pivot
            pivots = jnp.where(sub == k, pivot, pivots)
            uk, vk = row(u, k), row(v, k)
            ck = {j: row(c[j], k) for j in range(k + 1, PANEL)}
            if more:
                m = cn[k] * inv
                un = un - m * uk
                vn = vn - m * vk
                for j in ck:
                    cn[j] = cn[j] - m * ck[j]
            if k + 1 < PANEL:
                m = jnp.where(sub > k, c[k] * inv, 0.0)
                for j in ck:
                    c[j] = c[j] - m * ck[j]
                u = u - m * uk
                v = v - m * vk
        s = lax.rsqrt(pivots)
        s = s * (1.5 - 0.5 * pivots * s * s)
        u, v = u * s, v * s
        right[p] = v
        if p + 2 < groups:
            w = dot(u, jnp.concatenate([u, v], axis=1), ((0,), (0,)))
            for g in range(p + 2, groups):
                part = w[g * PANEL : (g + 1) * PANEL, :]
                left[g] = left[g] - part[:, :n]
                right[g] = right[g] - part[:, n:]
        if more:
            left[p + 1], right[p + 1] = un, vn
    return jnp.concatenate(right, axis=0)


def inverse_kernel(meta, mine, theirs, out, gram):
    r = meta[1]
    j, c = r // 2, r % 2
    n = gram.shape[0]
    half = n // 2
    pieces = mine.shape[0]
    height = mine.shape[1]
    for d in range(pieces):
        at = (j ^ d) * height
        gram[pl.ds(pl.multiple_of(c * half + at, 8), height), :] = mine[d]
        gram[pl.ds(pl.multiple_of((1 - c) * half + at, 8), height), :] = theirs[d]
    first = base_inverse(gram[:half, :half])
    out[:half, :half] = first
    out[:half, half:] = jnp.zeros((half, half), jnp.float32)
    below = dot(gram[half:, :half], first, ((1,), (1,)))
    second = base_inverse(gram[half:, half:] - dot(below, below, ((1,), (1,))))
    out[half:, half:] = second
    out[half:, :half] = -dot(second, dot(below, first))


def inverse_lower(meta, mine, theirs):
    n = mine.shape[2]
    vmem = pl.BlockSpec(memory_space=pltpu.VMEM)
    return pl.pallas_call(
        inverse_kernel,
        in_specs=[pl.BlockSpec(memory_space=pltpu.SMEM), vmem, vmem],
        out_specs=vmem,
        out_shape=jax.ShapeDtypeStruct((n, n), jnp.float32),
        scratch_shapes=[pltpu.VMEM((n, n), jnp.float32)],
    )(meta, mine, theirs)


def summed_inverse(meta, matrix):
    gram = dot(matrix, matrix, ((0,), (0,)))
    n_row, n_col = lax.axis_size("row"), lax.axis_size("col")
    n = gram.shape[0]
    r = lax.axis_index("row")
    j, c = r // 2, r % 2
    height = n // n_row
    pairs = n_row // 2
    gram = gram + swap(gram, "row", 1)
    parts = []
    for d in range(pairs):
        piece = lax.dynamic_slice_in_dim(gram, (c * pairs + (j ^ d)) * height, height, 0)
        parts.append(swap(piece, "row", 2 * d) if d else piece)
    piece = tree_sum(parts)
    parts = [piece] + [swap(piece, "col", d) for d in range(1, n_col)]
    piece = tree_sum(parts)
    parts = [piece] + [swap(piece, "row", 2 * d) for d in range(1, pairs)]
    mine = jnp.stack(parts)
    theirs = swap(mine, "row", 1)
    return inverse_lower(meta, mine, theirs)


def apply_factor(matrix, inverse):
    return dot(matrix, inverse, ((1,), (1,)))


def program(affinity, tile_rows, tile_cols, live_tiles, start):
    n_row = lax.axis_size("row")
    n_col = lax.axis_size("col")
    r = lax.axis_index("row")
    c = lax.axis_index("col")
    slot_count, tile_size = affinity.shape[0], affinity.shape[1]
    rows_local, vec_count = start.shape
    own_tiles = rows_local // tile_size
    width = vec_count // CHUNKS
    meta = jnp.stack([live_tiles[0], r, c, jnp.int32(n_row)]).astype(jnp.int32)

    def chunk(x, i):
        return x[:, i * width : (i + 1) * width]

    chunks = [chunk(start, i) for i in range(CHUNKS)]
    gathered = [gather_row(x) for x in chunks]

    live = (jnp.arange(slot_count) < live_tiles[0]).astype(jnp.float32)
    row_onehot = (jnp.arange(own_tiles * n_col)[:, None] == tile_rows[None, :]).astype(
        jnp.float32
    ) * live[None, :]
    row_sums = jnp.sum(affinity, axis=2, dtype=jnp.float32)
    degree_terms = dot(row_onehot, row_sums).reshape(n_col, own_tiles, tile_size)
    mine = []
    for d in range(n_col):
        block = lax.dynamic_index_in_dim(degree_terms, c ^ d, 0, keepdims=False)
        mine.append(swap(block, "col", d) if d else block)
    scaling_tiles = 1.0 / jnp.sqrt(1.0 + tree_sum(mine))
    near = jnp.stack([scaling_tiles] + [swap(scaling_tiles, "row", d) for d in range(2, n_row, 2)])
    factors = jnp.stack([near, swap(near, "row", 1)], axis=1).reshape(n_row * own_tiles, tile_size).T
    scaling = scaling_tiles.reshape(rows_local)[:, None]

    def image_of(pieces, basis, factors):
        parts = []
        for i in range(CHUNKS):
            theirs = forward(pieces[i])
            part = tile_products(
                meta, tile_rows, tile_cols, affinity, pieces[i], theirs, factors, n_col
            )
            parts.append(part)
        images = []
        for i in range(CHUNKS):
            total = scatter_col(parts[i])
            images.append(finish(scaling, basis[i], *total))
        chunks, scaled = zip(*images)
        return chunks, scaled, jnp.concatenate(chunks, axis=1)

    chunks, scaled, image = image_of(gathered, chunks, factors)
    firsts = []
    for _ in range(1, ITERS):
        gathered = [gather_row(x) for x in scaled]
        chunks, scaled, following = image_of(gathered, chunks, None)
        inner = summed_inverse(meta, image)
        first = apply_factor(image, inner)
        firsts.append(first)
        factor = dot(summed_inverse(meta, first), inner)
        image = apply_factor(following, factor)
        chunks = [chunk(image, i) for i in range(CHUNKS)]
        scaled = [scaling * x for x in chunks]
    pending = apply_factor(image, summed_inverse(meta, image))
    firsts.append(pending)
    basis = apply_factor(pending, summed_inverse(meta, pending))
    total_images = rows_local * n_row * n_col
    root = jnp.sqrt(jnp.float32(total_images))
    return (root * basis, root * jnp.stack(firsts, axis=0))


def solution(mesh):
    placed = (
        P(("col", "row"), None, None),
        P(("col", "row")),
        P(("col", "row")),
        P(("col", "row")),
        P(("col", "row"), None),
    )
    return jax.shard_map(
        program,
        mesh=mesh,
        in_specs=placed,
        out_specs=(P(("col", "row"), None), P(None, ("col", "row"), None)),
        check_vma=False,
    )
```

```python
import jax
import jax.numpy as jnp
from jax import lax
from jax.experimental import pallas as pl
from jax.experimental.pallas import tpu as pltpu
from jax.sharding import PartitionSpec as P

ITERS = 2
PANEL = 8
CHUNKS = 2


highest = lax.Precision.HIGHEST


def dot(a, b, dims=((1,), (0,))):
    return lax.dot_general(
        a, b, (dims, ((), ())), precision=highest, preferred_element_type=jnp.float32
    )


def swap(x, axis, d):
    n = lax.axis_size(axis)
    return lax.ppermute(x, axis, [(i, i ^ d) for i in range(n)])


def tree_sum(parts):
    while len(parts) > 1:
        parts = [parts[i] + parts[i + 1] for i in range(0, len(parts), 2)]
    return parts[0]


def gather_row(x):
    n = lax.axis_size("row")
    return [x] + [swap(x, "row", d) for d in range(2, n, 2)]


def forward(pieces):
    stacked = jnp.stack(pieces)
    return swap(stacked, "row", 1)


def product_kernel(n_row, n_col, own, scaled_here):
    def kernel(meta, rows, cols, aff, *refs):
        mine, theirs, refs = refs[: n_row // 2], refs[n_row // 2], refs[n_row // 2 + 1 :]
        if scaled_here:
            factors, refs = refs[0], refs[1:]
        outs, (split, total) = refs[:-2], refs[-2:]
        size, vecs = aff.shape[1], mine[0].shape[1]
        live, r, c = meta[0], meta[1], meta[2]
        total[...] = jnp.zeros(total.shape, jnp.float32)
        for d in range(n_row):
            first = (r ^ d) * own
            for t in range(own):
                at = slice(t * size, (t + 1) * size)
                x = theirs[d // 2, at, :] if d % 2 else mine[d // 2][at, :]
                if scaled_here:
                    x = x * factors[:, d * own + t : d * own + t + 1]
                high = x.astype(jnp.bfloat16)
                low = (x - high.astype(jnp.float32)).astype(jnp.bfloat16)
                split[first + t, :, :vecs] = high
                split[first + t, :, vecs:] = low

        def one(s):
            t = rows[s]
            q = ((t // own) ^ c) * own + t % own
            y = jnp.dot(aff[s], split[cols[s]], preferred_element_type=jnp.float32)
            total[q] = total[q] + (y[:, :vecs] + y[:, vecs:])

        def four(i, carry):
            for j in range(4):
                one(i * 4 + j)
            return carry

        def rest(s, carry):
            one(s)
            return carry

        whole = live // 4
        lax.fori_loop(0, whole, four, 0)
        lax.fori_loop(whole * 4, live, rest, 0)
        for o, qs in zip(outs, out_blocks(n_col)):
            for i, q in enumerate(qs):
                for t in range(own):
                    o[(i * own + t) * size : (i * own + t + 1) * size, :] = total[q * own + t]

    return kernel


def out_blocks(n_col):
    groups = [[0]]
    bit = n_col // 2
    while bit:
        groups.append([q for q in range(bit, n_col, 2 * bit)])
        bit //= 2
    return groups


def tile_products(meta, rows, cols, affinity, pieces, theirs, factors, n_col):
    n_row = 2 * len(pieces)
    size = affinity.shape[1]
    local, vecs = pieces[0].shape
    own = local // size
    vmem = pl.BlockSpec(memory_space=pltpu.VMEM)
    smem = pl.BlockSpec(memory_space=pltpu.SMEM)
    extra = [] if factors is None else [factors]
    return pl.pallas_call(
        product_kernel(n_row, n_col, own, factors is not None),
        in_specs=[smem] * 3 + [vmem] * (2 + len(pieces) + len(extra)),
        out_specs=[vmem] * len(out_blocks(n_col)),
        out_shape=[
            jax.ShapeDtypeStruct((len(g) * local, vecs), jnp.float32) for g in out_blocks(n_col)
        ],
        scratch_shapes=[
            pltpu.VMEM((n_row * own, size, 2 * vecs), jnp.bfloat16),
            pltpu.VMEM((n_col * own, size, vecs), jnp.float32),
        ],
    )(meta, rows, cols, affinity, *pieces, theirs, *extra)


def scatter_col(parts):
    parts = list(parts)
    local = parts[0].shape[0]
    n = len(parts)
    for step in range(n - 1):
        got = swap(parts[-1], "col", 1 << step)
        parts = parts[:-1]
        if len(parts) == 1:
            return parts[0], got
        count = got.shape[0] // local
        place = {i * 2: got[i * local : (i + 1) * local] for i in range(count)}
        groups = out_blocks(count * 2)[: len(parts)] if count > 1 else [[0]]
        new = []
        for p, g in zip(parts, groups):
            new.append(p + jnp.concatenate([place[q] for q in g]) if len(g) > 1 else p + place[g[0]])
        parts = new


def finish_kernel(scaling, basis, total, more, image, following):
    factor = jnp.broadcast_to(scaling[...], total.shape)
    value = factor * (factor * basis[...] + (total[...] + more[...]))
    image[...] = value
    following[...] = factor * value


def finish(scaling, basis, total, more):
    vmem = pl.BlockSpec(memory_space=pltpu.VMEM)
    shape = jax.ShapeDtypeStruct(total.shape, jnp.float32)
    return pl.pallas_call(
        finish_kernel, in_specs=[vmem] * 4, out_specs=[vmem] * 2, out_shape=[shape] * 2
    )(scaling, basis, total, more)


def base_inverse(a):
    n = a.shape[0]
    groups = n // PANEL
    sub = lax.broadcasted_iota(jnp.int32, (PANEL, n), 0)
    lane = lax.broadcasted_iota(jnp.int32, (PANEL, n), 1)

    def row(x, k):
        return jnp.broadcast_to(x[k : k + 1, :], x.shape)

    def col(x, k):
        return jnp.broadcast_to(x[:, k : k + 1], x.shape)

    left = [a[g * PANEL : (g + 1) * PANEL, :] for g in range(groups)]
    right = [(lane == sub + g * PANEL).astype(jnp.float32) for g in range(groups)]
    for p in range(groups):
        u, v = left[p], right[p]
        c = [col(u, p * PANEL + j) for j in range(PANEL)]
        more = p + 1 < groups
        if more:
            un, vn = left[p + 1], right[p + 1]
            cn = [col(un, p * PANEL + j) for j in range(PANEL)]
        pivots = jnp.ones((PANEL, n), jnp.float32)
        for k in range(PANEL):
            pivot = row(c[k], k)
            inv = 1.0 / pivot
            pivots = jnp.where(sub == k, pivot, pivots)
            uk, vk = row(u, k), row(v, k)
            ck = {j: row(c[j], k) for j in range(k + 1, PANEL)}
            if more:
                m = cn[k] * inv
                un = un - m * uk
                vn = vn - m * vk
                for j in ck:
                    cn[j] = cn[j] - m * ck[j]
            if k + 1 < PANEL:
                m = jnp.where(sub > k, c[k] * inv, 0.0)
                for j in ck:
                    c[j] = c[j] - m * ck[j]
                u = u - m * uk
                v = v - m * vk
        s = lax.rsqrt(pivots)
        s = s * (1.5 - 0.5 * pivots * s * s)
        u, v = u * s, v * s
        right[p] = v
        if p + 2 < groups:
            w = dot(u, jnp.concatenate([u, v], axis=1), ((0,), (0,)))
            for g in range(p + 2, groups):
                part = w[g * PANEL : (g + 1) * PANEL, :]
                left[g] = left[g] - part[:, :n]
                right[g] = right[g] - part[:, n:]
        if more:
            left[p + 1], right[p + 1] = un, vn
    return jnp.concatenate(right, axis=0)


def factor_inverse(gram):
    half = gram.shape[0] // 2
    first = base_inverse(gram[:half, :half])
    below = dot(gram[half:, :half], first, ((1,), (1,)))
    second = base_inverse(gram[half:, half:] - dot(below, below, ((1,), (1,))))
    corner = -dot(second, dot(below, first))
    return jnp.concatenate(
        [
            jnp.concatenate([first, jnp.zeros_like(first)], axis=1),
            jnp.concatenate([corner, second], axis=1),
        ],
        axis=0,
    )


def inverse_kernel(meta, mine, theirs, out, gram, held):
    r = meta[1]
    j, c = r // 2, r % 2
    count, n = gram.shape[0], gram.shape[1]
    half = n // 2
    pieces, height = mine.shape[0], mine.shape[2]
    for d in range(pieces):
        at = (j ^ d) * height
        for i in range(count):
            gram[i, pl.ds(pl.multiple_of(c * half + at, 8), height), :] = mine[d, i]
            gram[i, pl.ds(pl.multiple_of((1 - c) * half + at, 8), height), :] = theirs[d, i]

    def step(i, carry):
        @pl.when(i == 0)
        def _():
            held[...] = gram[0]

        @pl.when(i > 0)
        def _():
            held[...] = dot(dot(out[...], gram[i]), out[...], ((1,), (1,)))

        inverse = factor_inverse(held[...])

        @pl.when(i == 0)
        def _():
            out[...] = inverse

        @pl.when(i > 0)
        def _():
            out[...] = dot(inverse, out[...])

        return carry

    lax.fori_loop(0, count, step, 0)


def inverse_lower(meta, mine, theirs):
    count, n = mine.shape[1], mine.shape[3]
    vmem = pl.BlockSpec(memory_space=pltpu.VMEM)
    return pl.pallas_call(
        inverse_kernel,
        in_specs=[pl.BlockSpec(memory_space=pltpu.SMEM), vmem, vmem],
        out_specs=vmem,
        out_shape=jax.ShapeDtypeStruct((n, n), jnp.float32),
        scratch_shapes=[pltpu.VMEM((count, n, n), jnp.float32), pltpu.VMEM((n, n), jnp.float32)],
    )(meta, mine, theirs)


def summed_inverse(meta, matrices):
    gram = jnp.stack([dot(x, x, ((0,), (0,))) for x in matrices])
    n_row, n_col = lax.axis_size("row"), lax.axis_size("col")
    n = gram.shape[1]
    r = lax.axis_index("row")
    j, c = r // 2, r % 2
    height = n // n_row
    pairs = n_row // 2
    gram = gram + swap(gram, "row", 1)
    parts = []
    for d in range(pairs):
        piece = lax.dynamic_slice_in_dim(gram, (c * pairs + (j ^ d)) * height, height, 1)
        parts.append(swap(piece, "row", 2 * d) if d else piece)
    piece = tree_sum(parts)
    parts = [piece] + [swap(piece, "col", d) for d in range(1, n_col)]
    piece = tree_sum(parts)
    parts = [piece] + [swap(piece, "row", 2 * d) for d in range(1, pairs)]
    mine = jnp.stack(parts)
    theirs = swap(mine, "row", 1)
    return inverse_lower(meta, mine, theirs)


def apply_factor(matrix, inverse):
    return dot(matrix, inverse, ((1,), (1,)))


def program(affinity, tile_rows, tile_cols, live_tiles, start):
    n_row = lax.axis_size("row")
    n_col = lax.axis_size("col")
    r = lax.axis_index("row")
    c = lax.axis_index("col")
    slot_count, tile_size = affinity.shape[0], affinity.shape[1]
    rows_local, vec_count = start.shape
    own_tiles = rows_local // tile_size
    width = vec_count // CHUNKS
    meta = jnp.stack([live_tiles[0], r, c, jnp.int32(n_row)]).astype(jnp.int32)

    def chunk(x, i):
        return x[:, i * width : (i + 1) * width]

    chunks = [chunk(start, i) for i in range(CHUNKS)]
    gathered = [gather_row(x) for x in chunks]

    live = (jnp.arange(slot_count) < live_tiles[0]).astype(jnp.float32)
    row_onehot = (jnp.arange(own_tiles * n_col)[:, None] == tile_rows[None, :]).astype(
        jnp.float32
    ) * live[None, :]
    row_sums = jnp.sum(affinity, axis=2, dtype=jnp.float32)
    degree_terms = dot(row_onehot, row_sums).reshape(n_col, own_tiles, tile_size)
    mine = []
    for d in range(n_col):
        block = lax.dynamic_index_in_dim(degree_terms, c ^ d, 0, keepdims=False)
        mine.append(swap(block, "col", d) if d else block)
    scaling_tiles = 1.0 / jnp.sqrt(1.0 + tree_sum(mine))
    near = jnp.stack([scaling_tiles] + [swap(scaling_tiles, "row", d) for d in range(2, n_row, 2)])
    factors = jnp.stack([near, swap(near, "row", 1)], axis=1).reshape(n_row * own_tiles, tile_size).T
    scaling = scaling_tiles.reshape(rows_local)[:, None]

    def image_of(pieces, basis, factors):
        parts = []
        for i in range(CHUNKS):
            theirs = forward(pieces[i])
            part = tile_products(
                meta, tile_rows, tile_cols, affinity, pieces[i], theirs, factors, n_col
            )
            parts.append(part)
        images = []
        for i in range(CHUNKS):
            total = scatter_col(parts[i])
            images.append(finish(scaling, basis[i], *total))
        chunks, scaled = zip(*images)
        return chunks, scaled, jnp.concatenate(chunks, axis=1)

    chunks, scaled, image = image_of(gathered, chunks, factors)
    inner = summed_inverse(meta, [image])
    first = apply_factor(image, inner)
    firsts = [first]
    for k in range(1, ITERS):
        if k > 1:
            chunks = [chunk(first, i) for i in range(CHUNKS)]
            scaled = [scaling * x for x in chunks]
        gathered = [gather_row(x) for x in scaled]
        following = image_of(gathered, chunks, None)[2]
        raw = apply_factor(following, inner) if k == 1 else following
        first = apply_factor(raw, summed_inverse(meta, [first, raw]))
        firsts.append(first)
    basis = apply_factor(first, summed_inverse(meta, [first]))
    total_images = rows_local * n_row * n_col
    root = jnp.sqrt(jnp.float32(total_images))
    return (root * basis, root * jnp.stack(firsts, axis=0))


def solution(mesh):
    placed = (
        P(("col", "row"), None, None),
        P(("col", "row")),
        P(("col", "row")),
        P(("col", "row")),
        P(("col", "row"), None),
    )
    return jax.shard_map(
        program,
        mesh=mesh,
        in_specs=placed,
        out_specs=(P(("col", "row"), None), P(None, ("col", "row"), None)),
        check_vma=False,
    )
```
